32 devices in a mesh: row: 4 (over y, x), col: 4 (over z), tp: 2 (over core).
Axes of the slice: x: 2, y: 2, z: 4, core: 2. Of those that a mesh axis runs over, the one named last changes fastest.
Arguments:
- act_one: bfloat16 [4, 4, 256, 8192], P('row', 'col', None, 'tp'), may hold values from -6 to 6
- residual: bfloat16 [4, 4, 256, 2048], P('row', 'col', None, 'tp'), may hold values from -6 to 6
- upstream: bfloat16 [4, 4, 256, 8192], P('row', 'col', None, 'tp'), may hold values from -6 to 6
- stream_grad: bfloat16 [4, 4, 256, 256], P('row', 'col'), may hold values from -6 to 6
- token_ids: int32 [4, 4, 256], P('row', 'col'), may hold values from 0 to 31999, as said below
- shard_counts: int32 [4, 4], P('row', 'col'), may hold values from 1024 to 21463
- out_one: bfloat16 [4, 8192, 2048], P('col', 'tp', 'row'), may hold values from -6 to 6
- in_two: bfloat16 [4, 8192, 2048], P('row', 'tp', 'col'), may hold values from -6 to 6
- out_one_moment: float32 [4, 8192, 256], P('col', 'tp', 'row'), may hold values from -3 to 3
- in_two_moment: float32 [4, 8192, 256], P('row', 'tp', 'col'), may hold values from -3 to 3
Outputs:
- out_one_new: float32 [4, 8192, 256], P('col', 'tp', 'row')
- out_one_moment_new: float32 [4, 8192, 256], P('col', 'tp', 'row')
- in_two_new: float32 [4, 8192, 256], P('row', 'tp', 'col')
- in_two_moment_new: float32 [4, 8192, 256], P('row', 'tp', 'col')
The draws below stay inside these ranges and needn't reach their ends.
Inputs may be any that keep to these rules, and one draw needn't show every extreme that they name: `token_ids`: id 0 marks padding and appears only at the end of a path's tokens.
All inputs are finite; a program needn't handle non-finite values.
Results may differ from the reference program's by a relative error of at most 0.017.
Values may be sent and summed in bfloat16 or wider, within the bound.
No kernel may reach another device: no remote copies, remote signals or barrier semaphores. Data moves between devices by JAX's collectives and lax.ppermute only.
A program may use at most 128 MiB of HBM per device.

```python
import jax
import jax.numpy as jnp
from jax import lax

D = 2048
H = 8192
VOCAB = 32000
TOK = 256
COLS = 256
GR = 4
GC = 4
N_ROW = 4
N_COL = 4
N_TP = 2


def draw_token_ids(key, part):
    first_key, second_key = jax.random.split(jax.random.fold_in(key, 11))
    raw_ids = jax.random.randint(first_key, (GR, GC, TOK), 1, VOCAB)
    pad_len = jax.random.randint(second_key, (GR, GC, 1), 0, TOK // 2 + 1)
    position = jnp.arange(TOK)[None, None, :]
    return jnp.where(position < TOK - pad_len, raw_ids, 0).astype(jnp.int32)


def draw_shard_counts(key, part):
    base_draw = jax.random.randint(jax.random.fold_in(key, 23), (GR, GC), 64, 128)
    row_steps = jnp.arange(GR, dtype=jnp.int32)[:, None]
    col_steps = jnp.arange(GC, dtype=jnp.int32)[None, :]
    first_cell = (row_steps == 0) & (col_steps == 0)
    last_cell = (row_steps == GR - 1) & (col_steps == GC - 1)
    base_draw = jnp.where(first_cell, 64, base_draw)
    base_draw = jnp.where(last_cell, 127, base_draw)
    return (base_draw * (GR + 3 * row_steps) * (GC + 3 * col_steps)).astype(jnp.int32)


def steps_of(own_key, dims, cuts, least, high):
    level = 1.0
    for dim, blocks in cuts:
        draws = jax.random.uniform(jax.random.fold_in(jax.random.fold_in(own_key, 6), dim), (blocks,), jnp.float32, least / len(cuts), high / len(cuts))
        level = level * jnp.repeat(jnp.exp(draws), dims[dim] // blocks).reshape((-1,) + (1,) * (len(dims) - 1 - dim))
    return level


def noise(key, extent, spread, limit, cuts=(), kind=jnp.bfloat16):
    array = jax.random.normal(key, extent, jnp.float32) * spread
    if len(cuts) > 0:
        array = steps_of(key, extent, cuts, -0.22, 0.18) * array
    return jnp.clip(array, min=-limit, max=limit).astype(kind)


def setup_inputs(seed: int = 0) -> dict:
    key_of = jax.random.split(jax.random.key(seed), 11)
    act_one = noise(key_of[0], (GR, GC, TOK, H), 1.0, 6.0, ((0, 4), (1, 4), (3, 2)))
    residual = noise(key_of[1], (GR, GC, TOK, D), 1.0, 6.0, ((0, 4), (1, 4), (3, 2)))
    upstream = noise(key_of[2], (GR, GC, TOK, H), 1.0, 6.0, ((0, 4), (1, 4), (3, 2)))
    stream_grad = noise(key_of[3], (GR, GC, TOK, COLS), 1.0, 6.0, ((0, 4), (1, 4)))
    token_ids = draw_token_ids(jax.random.fold_in(key_of[10], 71), 0)
    shard_counts = draw_shard_counts(jax.random.fold_in(key_of[10], 71), 0)
    out_one = noise(key_of[6], (GC, H, D), 1.0, 6.0, ((0, 4), (1, 2), (2, 4)))
    in_two = noise(key_of[7], (GR, H, D), 1.0, 6.0, ((0, 4), (1, 2), (2, 4)))
    out_one_moment = noise(key_of[8], (GC, H, COLS), 0.5, 3.0, ((0, 4), (1, 2), (2, 4)), jnp.float32)
    in_two_moment = noise(key_of[9], (GR, H, COLS), 0.5, 3.0, ((0, 4), (1, 2), (2, 4)), jnp.float32)
    return dict(act_one=act_one, residual=residual, upstream=upstream, stream_grad=stream_grad, token_ids=token_ids, shard_counts=shard_counts, out_one=out_one, in_two=in_two, out_one_moment=out_one_moment, in_two_moment=in_two_moment)


inner_rate = 4.0
outer_rate = 0.7
momentum_decay = 0.9


def pick_columns(matrix, groups):
    rows = matrix.shape[0]
    return matrix.reshape(rows, groups, D // groups)[:, :, :COLS // groups].reshape(rows, COLS)


def hidden_groups(left, right, scale):
    count = left.shape[0]
    group = H // N_TP
    left_groups = left.reshape(count, N_TP, group).astype(jnp.float32)
    right_groups = right.reshape(N_TP, group, right.shape[1]).astype(jnp.float32)
    partial_value = jnp.einsum("tjh,jhd->jtd", left_groups, right_groups) * scale
    return jnp.sum(lax.optimization_barrier(partial_value.astype(jnp.bfloat16)).astype(jnp.float32), axis=0)


def path_grads(act_rows, resid_rows, up_rows, stream_rows, path_ids, first_weight, second_weight):
    scale_model = 1.0 / (D ** 0.5)
    scale_hidden = 1.0 / (H ** 0.5)
    keep = (path_ids != 0)[:, None]
    masked_up = jnp.where(keep, up_rows, jnp.zeros_like(up_rows))
    masked_stream = jnp.where(keep, stream_rows, jnp.zeros_like(stream_rows))
    summed = hidden_groups(act_rows, first_weight, scale_hidden)
    stream_rows_new = (resid_rows.astype(jnp.float32) + summed).astype(jnp.bfloat16)
    pre_second = jnp.dot(stream_rows_new, second_weight.T, preferred_element_type=jnp.float32) * scale_model
    squash = jax.nn.sigmoid(pre_second)
    slope = (masked_up.astype(jnp.float32) * squash * (1.0 + pre_second * (1.0 - squash))).astype(jnp.bfloat16)
    grad_two = jnp.dot(slope.T, pick_columns(stream_rows_new, N_COL), preferred_element_type=jnp.float32) * scale_model
    carried = hidden_groups(slope, pick_columns(second_weight, N_ROW), scale_model)
    stream_back = (masked_stream.astype(jnp.float32) + carried).astype(jnp.bfloat16)
    grad_one = jnp.dot(act_rows.T, stream_back, preferred_element_type=jnp.float32) * scale_hidden
    return grad_one, grad_two


def rounded_term(weight, grad):
    return lax.optimization_barrier((weight * inner_rate * grad).astype(jnp.bfloat16)).astype(jnp.float32)


def outer_step(picked, moment, summed, total):
    delta = summed / total[:, None, None]
    moment_new = momentum_decay * moment + delta
    fresh = picked.astype(jnp.float32) - outer_rate * (delta + momentum_decay * moment_new)
    return fresh, moment_new


def reference(act_one, residual, upstream, stream_grad, token_ids, shard_counts, out_one, in_two, out_one_moment, in_two_moment):
    counts = shard_counts.astype(jnp.float32)
    start = (jnp.zeros((GC, H, COLS), jnp.float32), jnp.zeros((GR, H, COLS), jnp.float32))

    def visit(carried, path_index):
        sum_one, sum_two = carried
        row_at = path_index // GC
        col_at = path_index % GC
        grads = path_grads(act_one[row_at, col_at], residual[row_at, col_at], upstream[row_at, col_at], stream_grad[row_at, col_at], token_ids[row_at, col_at], out_one[col_at], in_two[row_at])
        weight = counts[row_at, col_at]
        sum_one = sum_one.at[col_at].add(rounded_term(weight, grads[0]))
        sum_two = sum_two.at[row_at].add(rounded_term(weight, grads[1]))
        return (sum_one, sum_two), None

    sums, _ = lax.scan(visit, start, jnp.arange(GR * GC, dtype=jnp.int32))
    total_one = jnp.sum(counts, axis=0)
    total_two = jnp.sum(counts, axis=1)
    picked_one = jax.vmap(lambda matrix: pick_columns(matrix, N_ROW))(out_one)
    picked_two = jax.vmap(lambda matrix: pick_columns(matrix, N_COL))(in_two)
    out_one_new, out_one_moment_new = outer_step(picked_one, out_one_moment, sums[0], total_one)
    in_two_new, in_two_moment_new = outer_step(picked_two, in_two_moment, sums[1], total_two)
    return out_one_new, out_one_moment_new, in_two_new, in_two_moment_new
```

```python
import math

import jax
import jax.numpy as jnp
from jax import lax
from jax.sharding import PartitionSpec as P

inner_rate = 4.0
outer_rate = 0.7
momentum_decay = 0.9


f32 = jnp.float32
bf16 = jnp.bfloat16


def swap(values, axis, step):
    if step == 0:
        return values
    count = lax.axis_size(axis)
    return lax.ppermute(values, axis, [(i, i ^ step) for i in range(count)])


def arrange(pieces, key):
    bit = 1
    while bit < len(pieces):
        flip = (key & bit) != 0
        pieces = [jnp.where(flip, pieces[i ^ bit], pieces[i]) for i in range(len(pieces))]
        bit *= 2
    return pieces


def part(values, index, size, dim):
    return lax.dynamic_slice_in_dim(values, index * size, size, dim)


def outer_step(piece, moment, delta):
    moment_new = momentum_decay * moment + delta
    fresh = piece.astype(f32) - outer_rate * (delta + momentum_decay * moment_new)
    return fresh.T[None], moment_new.T[None]


def on_device(
    act_one,
    residual,
    upstream,
    stream_grad,
    token_ids,
    shard_counts,
    out_one,
    in_two,
    out_one_moment,
    in_two_moment,
):
    n_r, n_c, n_t = (lax.axis_size(a) for a in ("row", "col", "tp"))
    r, c, k = (lax.axis_index(a) for a in ("row", "col", "tp"))
    if n_r != n_c or (n_r & (n_r - 1)) or (n_t & (n_t - 1)):
        raise ValueError("mesh")
    act = act_one[0, 0]
    first_store = out_one[0]
    second_store = in_two[0]
    tok, hid = act.shape
    wide = residual.shape[3] * n_t
    cols = stream_grad.shape[3]
    block = wide // n_r
    sub = block // n_t
    chunk = hid // n_c
    share = cols // n_r
    scale_model = 1.0 / math.sqrt(wide)
    scale_hidden = 1.0 / math.sqrt(hid * n_t)

    weights = [
        swap(part(second_store, c ^ m, chunk, 0), "col", m) for m in range(n_c)
    ]
    acts = [swap(act, "row", j) for j in range(n_r)]
    keep = (token_ids[0, 0] != 0)[:, None]
    up = jnp.where(keep, upstream[0, 0], jnp.zeros_like(upstream[0, 0]))
    ups = [swap(part(up, c ^ m, chunk, 1), "col", m) for m in range(n_c)]
    count = shard_counts[0]
    weight_col = [swap(count, "col", m).astype(f32)[0] for m in range(n_c)]
    weight_row = [swap(count, "row", j).astype(f32)[0] for j in range(n_r)]
    total_one = sum(weight_row)
    total_two = sum(weight_col)

    resid_all = jnp.stack([swap(residual[0, 0], "tp", t) for t in range(n_t)])
    per = wide // n_t
    resid = []
    for j in range(n_r):
        start = (r ^ j) * block + k * sub
        resid.append(
            lax.dynamic_slice(resid_all, ((start // per) ^ k, 0, start % per), (1, tok, sub))[0]
        )

    mine = []
    for j in range(n_r):
        partial_value = (
            jnp.dot(acts[j], first_store, preferred_element_type=f32) * scale_hidden
        ).astype(bf16)
        summed = part(partial_value, k, sub, 1).astype(f32)
        for t in range(1, n_t):
            summed += swap(part(partial_value, k ^ t, sub, 1), "tp", t).astype(f32)
        arrived = swap(summed.astype(bf16), "row", j)
        mine.append((resid[j].astype(f32) + arrived.astype(f32)).astype(bf16))
    own = jnp.concatenate(mine, axis=1)

    halves = {0: own}
    bit = n_c // 2
    while bit:
        for m in list(halves):
            halves[m | bit] = swap(halves[m], "col", bit)
        bit //= 2
    weight = jnp.concatenate(arrange(weights, c ^ r), axis=1)
    picked = weight.reshape(chunk, n_r, block)[:, :, :share].reshape(chunk, cols)

    grad_two = 0.0
    carried = []
    for m in range(n_c):
        around = arrange([swap(halves[m], "tp", t).reshape(tok, n_r, sub) for t in range(n_t)], k)
        stream = jnp.stack(around, axis=2).reshape(tok, wide)
        pre = (
            jnp.einsum("td,hd->th", stream, weight, preferred_element_type=f32) * scale_model
        )
        squash = jax.nn.sigmoid(pre)
        slope = (ups[m].astype(f32) * squash * (1.0 + pre * (1.0 - squash))).astype(bf16)
        carried.append(
            (
                jnp.einsum("hd,th->dt", picked, slope, preferred_element_type=f32) * scale_model
            ).astype(bf16)
        )
        stream_picked = stream.reshape(tok, n_c, block)[:, :, :share].reshape(tok, cols)
        grad_two += jnp.einsum(
            "td,th->dh", stream_picked, slope, preferred_element_type=f32
        ) * (weight_col[m] * (inner_rate * scale_model) / total_two)

    stream_rows = jnp.where(keep, stream_grad[0, 0], jnp.zeros_like(stream_grad[0, 0])).T
    stream_rows = jnp.concatenate(
        arrange([stream_rows[j * share : (j + 1) * share] for j in range(n_r)], r), axis=0
    )
    rows = cols // n_t
    stream_rows = part(stream_rows, k, rows, 0)
    partial_value = jnp.concatenate(carried, axis=1)
    summed = part(partial_value, k, rows, 0).astype(f32)
    for t in range(1, n_t):
        summed += swap(part(partial_value, k ^ t, rows, 0), "tp", t).astype(f32)
    summed = summed.astype(bf16)
    back = stream_rows.astype(f32)
    for m in range(n_c):
        back += swap(summed[:, m * tok : (m + 1) * tok], "col", m).astype(f32)
    back = (back * (weight_row[0] * (inner_rate * scale_hidden) / total_one)).astype(bf16)
    back = jnp.concatenate(arrange([swap(back, "tp", t) for t in range(n_t)], k), axis=0)
    delta_one = 0.0
    for j in range(n_r):
        group = swap(back[j * share : (j + 1) * share], "row", j)
        delta_one += jnp.dot(group, acts[j], preferred_element_type=f32)

    grad_two = grad_two.astype(bf16)
    arrived = [swap(part(grad_two, r ^ c ^ m, share, 0), "col", m) for m in range(n_c)]
    delta_two = jnp.concatenate(arrange(arrived, c), axis=1).astype(f32)

    fresh_one = outer_step(first_store[:, :share].T, out_one_moment[0].T, delta_one)
    fresh_two = outer_step(second_store[:, :share].T, in_two_moment[0].T, delta_two)
    return fresh_one + fresh_two


def solution(mesh):
    return jax.shard_map(
        on_device,
        mesh=mesh,
        in_specs=(
            P("row", "col", None, "tp"),
            P("row", "col", None, "tp"),
            P("row", "col", None, "tp"),
            P("row", "col", None, None),
            P("row", "col", None),
            P("row", "col"),
            P("col", "tp", "row"),
            P("row", "tp", "col"),
            P("col", "tp", "row"),
            P("row", "tp", "col"),
        ),
        out_specs=(
            P("col", "tp", "row"),
            P("col", "tp", "row"),
            P("row", "tp", "col"),
            P("row", "tp", "col"),
        ),
        check_vma=False,
    )
```

```python
import functools
import math

import jax
import jax.numpy as jnp
from jax import lax
from jax.experimental import pallas as pl
from jax.experimental.pallas import tpu as pltpu
from jax.sharding import PartitionSpec as P


inner_rate = 4.0
outer_rate = 0.7
momentum_decay = 0.9


f32 = jnp.float32
bf16 = jnp.bfloat16


def swap(values, axis, step):
    if step == 0:
        return values
    count = lax.axis_size(axis)
    return lax.ppermute(values, axis, [(i, i ^ step) for i in range(count)])


def after(values, *others):
    return lax.optimization_barrier((values,) + others)[0]


def arrange(pieces, key):
    bit = 1
    while bit < len(pieces):
        flip = (key & bit) != 0
        pieces = [jnp.where(flip, pieces[i ^ bit], pieces[i]) for i in range(len(pieces))]
        bit *= 2
    return pieces


def part(values, index, size, dim):
    return lax.dynamic_slice_in_dim(values, index * size, size, dim)


def nt(left, right):
    return lax.dot_general(left, right, (((1,), (1,)), ((), ())), preferred_element_type=f32)


def slope_of(pre, up):
    squash = jax.nn.sigmoid(pre)
    return (up.astype(f32) * squash * (1.0 + pre * (1.0 - squash))).astype(bf16)


def updated(piece, moment, delta):
    moment_new = momentum_decay * moment + delta
    fresh = piece.astype(f32) - outer_rate * (delta + momentum_decay * moment_new)
    return fresh, moment_new


vmem = pl.BlockSpec(memory_space=pltpu.VMEM)
smem = pl.BlockSpec(memory_space=pltpu.SMEM)


def kernel_call(kernel, outs, args, flops=0, scratch=(), exps=0):
    outs = [jax.ShapeDtypeStruct(shape, kind) for shape, kind in outs]
    size = lambda x: math.prod(x.shape) * jnp.dtype(x.dtype).itemsize
    return pl.pallas_call(
        kernel,
        in_specs=[smem if x.size < 16 else vmem for x in args],
        out_specs=[vmem] * len(outs),
        out_shape=outs,
        scratch_shapes=list(scratch),
        compiler_params=pltpu.CompilerParams(vmem_limit_bytes=16 << 20),
        cost_estimate=pl.CostEstimate(
            flops=flops,
            bytes_accessed=sum(size(x) for x in outs) + sum(size(x) for x in args),
            transcendentals=exps,
        ),
    )(*args)


def join_kernel(count, *refs):
    base, arrived, out = refs[:count], refs[count : 2 * count], refs[2 * count]
    sub = base[0].shape[1]
    for j in range(count):
        total = base[j][...].astype(f32) + arrived[j][...].astype(f32)
        out[:, j * sub : (j + 1) * sub] = total.astype(bf16)


def join(base, arrived):
    tok, sub = base[0].shape
    count = len(base)
    outs = [((tok, count * sub), bf16)]
    return kernel_call(functools.partial(join_kernel, count), outs, base + arrived)[0]


def pick_kernel(share, key, *refs):
    pieces, out = refs[:-1], refs[-1]
    for m, piece in enumerate(pieces):
        at = pl.ds(pl.multiple_of((m ^ key[0]) * share, share), share)
        out[at, :] = piece[:, :128].T[:share]


def pick(key, pieces, share):
    outs = [((len(pieces) * share, pieces[0].shape[0]), bf16)]
    return kernel_call(functools.partial(pick_kernel, share), outs, [key] + pieces)[0]


def pre_kernel(scale, share, key, same, other, *refs):
    pieces, (pre, front, stream) = refs[:-3], refs[-3:]
    block = pieces[0].shape[1]
    sub = block // 2
    for m in range(len(pieces)):
        at = pl.ds(pl.multiple_of((m ^ key[0]) * sub, sub), sub)
        mine = m * block + key[1] * sub
        theirs = m * block + (1 - key[1]) * sub
        stream[:, pl.ds(pl.multiple_of(mine, sub), sub)] = same[:, at]
        stream[:, pl.ds(pl.multiple_of(theirs, sub), sub)] = other[:, at]
    for m in range(len(pieces)):
        front[m * share : (m + 1) * share, :] = stream[:, m * block : m * block + 128].T[:share]
    total = nt(pieces[0][...], stream[:, :block])
    for m in range(1, len(pieces)):
        total += nt(pieces[m][...], stream[:, m * block : (m + 1) * block])
    pre[...] = total * scale


def pre_second(key, same, other, pieces, share, scale):
    tok = same.shape[0]
    chunk, block = pieces[0].shape
    count = len(pieces)
    return kernel_call(
        functools.partial(pre_kernel, scale, share),
        [((chunk, tok), f32), ((count * share, tok), bf16)],
        [key, same, other] + pieces,
        flops=2 * tok * chunk * count * block,
        scratch=[pltpu.VMEM((tok, count * block), bf16)],
    )


def slope_kernel(scale, rate, step, groups, pre, up, picked, front, *refs):
    last = groups > 1
    before, carried, seen = refs[: -2 - groups], refs[-2 - groups], refs[-1 - groups]
    totals = refs[-groups:]
    share = totals[0].shape[0]
    chunk = pre.shape[0]
    digits = up[chunk : chunk + 16, :].astype(f32)
    number = digits[0:1] + 256.0 * digits[1:2] + 65536.0 * digits[2:3]
    seen[...] = number + before[0][...] if before else number
    weight = number * rate
    if last:
        norm = 1.0 / seen[...]
    sums = None
    for start in range(0, chunk, step):
        rows = slice(start, start + step)
        slope = slope_of(pre[rows, :], up[rows, :])
        add = jnp.dot(picked[:, rows], slope, preferred_element_type=f32)
        sums = add if sums is None else sums + add
        grad = nt(front[...], slope) * weight[:, :step]
        if before:
            grad += before[1][:, rows]
        if last:
            grad = (grad * norm[:, :step]).astype(bf16)
        for m, total in enumerate(totals):
            total[:, rows] = grad[m * share : (m + 1) * share]
    carried[...] = (sums * scale).astype(bf16)


def level_two(pre, up, picked, front, before, scale, rate, groups):
    chunk, tok = pre.shape
    cols = picked.shape[0]
    step = min(math.gcd(chunk, 256), tok)
    return kernel_call(
        functools.partial(slope_kernel, scale, rate, step, groups),
        [((cols, tok), bf16), ((1, tok), f32)]
        + [((cols // groups, chunk), bf16 if groups > 1 else f32)] * groups,
        [pre, up, picked, front] + before,
        flops=4 * tok * cols * chunk,
        exps=tok * chunk,
    )


def add_kernel(*refs):
    total = refs[0][...].astype(f32)
    for ref in refs[1:-1]:
        total += ref[...].astype(f32)
    refs[-1][...] = total.astype(bf16)


def add_up(pieces):
    return kernel_call(add_kernel, [(pieces[0].shape, bf16)], pieces)[0]


def back_kernel(share, mine, theirs, stream, rate, *groups):
    total = stream[...].astype(f32) + mine[...].astype(f32) + theirs[...].astype(f32)
    total = (total * rate[0]).astype(bf16)
    for j, group in enumerate(groups):
        group[...] = total[j * share : (j + 1) * share]


def back_groups(mine, theirs, stream, rate, share):
    cols, tok = stream.shape
    return kernel_call(
        functools.partial(back_kernel, share),
        [((share, tok), bf16)] * (cols // share),
        [mine, theirs, stream, rate],
    )


def outer_kernel(key, piece, moment, *refs):
    deltas, (fresh, moment_new) = refs[:-2], refs[-2:]
    chunk = deltas[0].shape[1]
    for m, delta in enumerate(deltas):
        at = pl.ds(pl.multiple_of((m ^ key[0]) * chunk, chunk), chunk)
        fresh[:, at], moment_new[:, at] = updated(
            piece[:, at], moment[:, at], delta[...].astype(f32)
        )


def outer_chunks(key, piece, moment, deltas):
    outs = [(piece.shape, f32)] * 2
    return kernel_call(outer_kernel, outs, [key, piece, moment] + deltas)


def hold_kernel(*refs):
    out, start = refs[-1], 0
    for piece in refs[:-1]:
        out[start : start + piece.shape[0], :] = piece[...]
        start += piece.shape[0]


def hold(pieces):
    rows = sum(x.shape[0] for x in pieces)
    return kernel_call(hold_kernel, [((rows, pieces[0].shape[1]), bf16)], pieces)[0]


def finish_kernel(step, *refs):
    groups, (acts, piece, moment, fresh, moment_new) = refs[:-5], refs[-5:]
    group = jnp.concatenate([g[...] for g in groups], axis=1)

    @pl.loop(0, piece.shape[1] // step)
    def _(i):
        at = pl.ds(pl.multiple_of(i * step, step), step)
        delta = jnp.dot(group, acts[:, at], preferred_element_type=f32)
        fresh[:, at], moment_new[:, at] = updated(piece[:, at], moment[:, at], delta)


def finish(groups, acts, piece, moment):
    share, hid = piece.shape
    return kernel_call(
        functools.partial(finish_kernel, math.gcd(hid, 1024)),
        [((share, hid), f32)] * 2,
        groups + [acts, piece, moment],
        flops=2 * share * hid * acts.shape[0],
    )


def on_device(
    act_one,
    residual,
    upstream,
    stream_grad,
    token_ids,
    shard_counts,
    out_one,
    in_two,
    out_one_moment,
    in_two_moment,
):
    n_r, n_c, n_t = (lax.axis_size(a) for a in ("row", "col", "tp"))
    r, c, k = (lax.axis_index(a) for a in ("row", "col", "tp"))
    if n_r != n_c or (n_r & (n_r - 1)) or (n_t & (n_t - 1)):
        raise ValueError("mesh")
    act = act_one[0, 0]
    first_store = out_one[0]
    second_store = in_two[0]
    tok, hid = act.shape
    wide = residual.shape[3] * n_t
    cols = stream_grad.shape[3]
    block = wide // n_r
    sub = block // n_t
    chunk = hid // n_c
    share = cols // n_r
    scale_model = 1.0 / math.sqrt(wide)
    scale_hidden = 1.0 / math.sqrt(hid * n_t)
    kernels = n_t == 2 and sub % 128 == 0 and share <= 128 and chunk % 256 == 0

    farthest = sorted(range(1, n_c), reverse=True)
    sent = [part(second_store, c ^ m, chunk, 0) for m in farthest]
    weights = {m: swap(piece, "col", m) for m, piece in zip(farthest, sent)}
    act_out = after(act, *sent)
    mine = after(residual[0, 0], *sent)
    resid_all = [swap(mine, "tp", t) for t in range(n_t)]
    gate = resid_all[-1]
    weights[0] = part(after(second_store, gate), c, chunk, 0)
    acts = {0: [act]}
    for j in sorted(range(1, n_r), key=lambda j: j.bit_count()):
        bits = [1 << b for b in range(n_r.bit_length()) if j >> b & 1]
        if len(bits) == 1:
            acts[j] = [swap(act_out, "row", j)]
        else:
            low, high = bits[0], bits[-1]
            lower = jnp.concatenate(acts[j ^ low])[: tok // 2]
            upper = jnp.concatenate(acts[j ^ high])[tok // 2 :]
            acts[j] = [swap(lower, "row", low), swap(upper, "row", high)]
    keep = (after(token_ids[0, 0], gate) != 0)[:, None]
    up = after(upstream[0, 0], gate)
    up = jnp.where(keep, up, jnp.zeros_like(up)).T
    number = shard_counts[0, 0]
    digits = jnp.stack([(number >> s) & 255 for s in (0, 8, 16)]).astype(bf16)
    digits = jnp.pad(jnp.broadcast_to(digits[:, None], (3, tok)), ((0, 13), (0, 0)))
    sent_ups = [
        jnp.concatenate([part(up, c ^ m, chunk, 0), digits], axis=0) for m in range(n_c)
    ]
    ups = [swap(sent_ups[m], "col", m) for m in range(n_c)]

    resid_all = jnp.stack(resid_all)
    per = wide // n_t
    resid = []
    for j in range(n_r):
        start = (r ^ j) * block + k * sub
        resid.append(
            lax.dynamic_slice(resid_all, ((start // per) ^ k, 0, start % per), (1, tok, sub))[0]
        )

    stream_rows = after(stream_grad[0, 0], gate)
    stream_rows = jnp.where(keep, stream_rows, jnp.zeros_like(stream_rows)).T
    stream_rows = jnp.concatenate(
        arrange([stream_rows[j * share : (j + 1) * share] for j in range(n_r)], r), axis=0
    )
    piece_one = after(first_store, gate)[:, :share].T
    piece_two = after(second_store, gate)[:, :share].T
    ready = [weights[0], stream_rows, piece_one, piece_two] + resid + sent_ups

    mine = []
    for j in range(n_r):
        behind = ready if j else [gate]
        partial_value = [
            jnp.dot(after(a, *behind), first_store, preferred_element_type=f32)
            for a in acts[j]
        ]
        partial_value = jnp.concatenate([(p * scale_hidden).astype(bf16) for p in partial_value])
        if j == 0:
            ready.append(partial_value)
        summed = part(partial_value, k, sub, 1).astype(f32)
        for t in range(1, n_t):
            summed += swap(part(partial_value, k ^ t, sub, 1), "tp", t).astype(f32)
        mine.append(swap(summed.astype(bf16), "row", j))
    if kernels:
        own = join(resid, mine)
    else:
        own = jnp.concatenate([b.astype(f32) + a.astype(f32) for b, a in zip(resid, mine)], axis=1)
        own = own.astype(bf16)

    count = after(shard_counts[0], own)
    weight_row = [swap(count, "row", j).astype(f32) for j in range(n_r)]
    total_one = sum(weight_row)

    halves = {0: own}
    bit = n_c // 2
    while bit:
        for m in list(halves):
            halves[m | bit] = swap(halves[m], "col", bit)
        bit //= 2
    pieces = [weights[m] for m in range(n_c)]
    key = jnp.stack([c ^ r, k]).astype(jnp.int32)
    if kernels:
        picked = pick(key, pieces, share)
    else:
        picked = jnp.concatenate(arrange([p[:, :share].T for p in pieces], c ^ r), axis=0)
        weight = jnp.concatenate(arrange(pieces, c ^ r), axis=1)

    sums = []
    total_two = 0.0
    arrived = []
    for m in range(n_c):
        streams = [swap(halves[m], "tp", t) for t in range(n_t)]
        if kernels:
            pre, front = pre_second(
                key, streams[0], streams[1], pieces, share, scale_model
            )
            carried, *sums = level_two(
                pre,
                ups[m],
                picked,
                front,
                sums,
                scale_model,
                inner_rate * scale_model,
                n_c if m == n_c - 1 else 1,
            )
            grad_two = sums[1:]
        else:
            around = arrange([s.reshape(tok, n_r, sub) for s in streams], k)
            stream = jnp.stack(around, axis=2).reshape(tok, wide)
            slope = slope_of(nt(weight, stream) * scale_model, ups[m][:chunk])
            given = ups[m][chunk : chunk + 3, 0].astype(f32)
            given = given[0] + 256.0 * given[1] + 65536.0 * given[2]
            total_two += given
            carried = jnp.dot(picked, slope, preferred_element_type=f32)
            carried = (carried * scale_model).astype(bf16)
            front = stream.reshape(tok, n_c, block)[:, :, :share]
            front = jnp.stack(arrange([front[:, j] for j in range(n_c)], c ^ r), axis=1)
            grad = nt(front.reshape(tok, cols).T, slope) * (given * (inner_rate * scale_model))
            sums.append(grad)
            grad_two = (sum(sums) / total_two).astype(bf16)
            grad_two = [grad_two[m * share : (m + 1) * share] for m in range(n_c)]
        arrived.append(swap(carried, "col", m))

    rate = weight_row[0] * (inner_rate * scale_hidden) / total_one
    if kernels:
        partial_value = add_up(arrived)
        theirs = swap(partial_value, "tp", 1)
        groups = back_groups(partial_value, theirs, stream_rows, rate, share)
    else:
        partial_value = sum(a.astype(f32) for a in arrived).astype(bf16)
        back = stream_rows.astype(f32)
        for t in range(n_t):
            back += swap(partial_value, "tp", t).astype(f32)
        back = (back * rate).astype(bf16)
        groups = [back[j * share : (j + 1) * share] for j in range(n_r)]
    groups = [swap(groups[j], "row", j) for j in range(n_r)]

    deltas = [swap(grad_two[m], "col", m) for m in range(n_c)]
    moment_one, moment_two = out_one_moment[0].T, in_two_moment[0].T
    if kernels:
        held = hold([a for j in range(n_r) for a in acts[j]])
        own_key = jnp.stack([c, k]).astype(jnp.int32)
        fresh_two = outer_chunks(own_key, piece_two, moment_two, deltas)
        fresh_one = finish(groups, held, piece_one, moment_one)
    else:
        delta_two = jnp.concatenate(arrange(deltas, c), axis=1).astype(f32)
        fresh_two = updated(piece_two, moment_two, delta_two)
        delta_one = sum(
            jnp.dot(groups[j], jnp.concatenate(acts[j]), preferred_element_type=f32)
            for j in range(n_r)
        )
        fresh_one = updated(piece_one, moment_one, delta_one)
    return tuple(x.T[None] for x in tuple(fresh_one) + tuple(fresh_two))


def solution(mesh):
    return jax.shard_map(
        on_device,
        mesh=mesh,
        in_specs=(
            P("row", "col", None, "tp"),
            P("row", "col", None, "tp"),
            P("row", "col", None, "tp"),
            P("row", "col", None, None),
            P("row", "col", None),
            P("row", "col"),
            P("col", "tp", "row"),
            P("row", "tp", "col"),
            P("col", "tp", "row"),
            P("row", "tp", "col"),
        ),
        out_specs=(
            P("col", "tp", "row"),
            P("col", "tp", "row"),
            P("row", "tp", "col"),
            P("row", "tp", "col"),
        ),
        check_vma=False,
    )
```

```python
import functools
import math

import jax
import jax.numpy as jnp
from jax import lax
from jax.experimental import pallas as pl
from jax.experimental.pallas import tpu as pltpu
from jax.sharding import PartitionSpec as P


inner_rate = 4.0
outer_rate = 0.7
momentum_decay = 0.9


f32 = jnp.float32
bf16 = jnp.bfloat16


def swap(values, axis, step):
    if step == 0:
        return values
    count = lax.axis_size(axis)
    return lax.ppermute(values, axis, [(i, i ^ step) for i in range(count)])


def after(values, *others):
    return lax.optimization_barrier((values,) + others)[0]


def arrange(pieces, key):
    bit = 1
    while bit < len(pieces):
        flip = (key & bit) != 0
        pieces = [jnp.where(flip, pieces[i ^ bit], pieces[i]) for i in range(len(pieces))]
        bit *= 2
    return pieces


def part(values, index, size, dim):
    return lax.dynamic_slice_in_dim(values, index * size, size, dim)


def nt(left, right):
    return lax.dot_general(left, right, (((1,), (1,)), ((), ())), preferred_element_type=f32)


def slope_of(pre, up):
    squash = jax.nn.sigmoid(pre)
    return (up.astype(f32) * squash * (1.0 + pre * (1.0 - squash))).astype(bf16)


def updated(piece, moment, delta):
    moment_new = momentum_decay * moment + delta
    fresh = piece.astype(f32) - outer_rate * (delta + momentum_decay * moment_new)
    return fresh, moment_new


vmem = pl.BlockSpec(memory_space=pltpu.VMEM)
smem = pl.BlockSpec(memory_space=pltpu.SMEM)


def kernel_call(kernel, outs, args, flops=0, scratch=(), exps=0, outs_in=pltpu.VMEM):
    outs = [jax.ShapeDtypeStruct(shape, kind) for shape, kind in outs]
    size = lambda x: math.prod(x.shape) * jnp.dtype(x.dtype).itemsize
    return pl.pallas_call(
        kernel,
        in_specs=[smem if x.size < 16 else vmem for x in args],
        out_specs=[pl.BlockSpec(memory_space=outs_in)] * len(outs),
        out_shape=outs,
        scratch_shapes=list(scratch),
        compiler_params=pltpu.CompilerParams(vmem_limit_bytes=16 << 20),
        cost_estimate=pl.CostEstimate(
            flops=flops,
            bytes_accessed=sum(size(x) for x in outs) + sum(size(x) for x in args),
            transcendentals=exps,
        ),
    )(*args)


def join_kernel(count, *refs):
    base, arrived, out = refs[:count], refs[count : 2 * count], refs[2 * count]
    sub = base[0].shape[1]
    for j in range(count):
        total = base[j][...].astype(f32) + arrived[j][...].astype(f32)
        out[:, j * sub : (j + 1) * sub] = total.astype(bf16)


def join(base, arrived):
    tok, sub = base[0].shape
    count = len(base)
    outs = [((tok, count * sub), bf16)]
    return kernel_call(functools.partial(join_kernel, count), outs, base + arrived)[0]


def pick_kernel(share, key, *refs):
    pieces, out = refs[:-1], refs[-1]
    for m, piece in enumerate(pieces):
        at = pl.ds(pl.multiple_of((m ^ key[0]) * share, share), share)
        out[at, :] = piece[:, :128].T[:share]


def pick(key, pieces, share):
    outs = [((len(pieces) * share, pieces[0].shape[0]), bf16)]
    return kernel_call(functools.partial(pick_kernel, share), outs, [key] + pieces)[0]


def lead_kernel(share, store, out):
    out[...] = store[...].T[:share]


def lead(store, share):
    hid = store.shape[0]
    step = math.gcd(hid, 512)
    return pl.pallas_call(
        functools.partial(lead_kernel, share),
        grid=(hid // step,),
        in_specs=[pl.BlockSpec((step, 128), lambda i: (i, 0))],
        out_specs=pl.BlockSpec((share, step), lambda i: (0, i)),
        out_shape=jax.ShapeDtypeStruct((share, hid), bf16),
        name="lead",
    )(store)


def pre_kernel(scale, share, key, same, other, *refs):
    pieces, (pre, front, stream) = refs[:-3], refs[-3:]
    block = pieces[0].shape[1]
    sub = block // 2
    for m in range(len(pieces)):
        at = pl.ds(pl.multiple_of((m ^ key[0]) * sub, sub), sub)
        mine = m * block + key[1] * sub
        theirs = m * block + (1 - key[1]) * sub
        stream[:, pl.ds(pl.multiple_of(mine, sub), sub)] = same[:, at]
        stream[:, pl.ds(pl.multiple_of(theirs, sub), sub)] = other[:, at]
    for m in range(len(pieces)):
        front[m * share : (m + 1) * share, :] = stream[:, m * block : m * block + 128].T[:share]
    total = nt(pieces[0][...], stream[:, :block])
    for m in range(1, len(pieces)):
        total += nt(pieces[m][...], stream[:, m * block : (m + 1) * block])
    pre[...] = total * scale


def pre_second(key, same, other, pieces, share, scale):
    tok = same.shape[0]
    chunk, block = pieces[0].shape
    count = len(pieces)
    return kernel_call(
        functools.partial(pre_kernel, scale, share),
        [((chunk, tok), f32), ((count * share, tok), bf16)],
        [key, same, other] + pieces,
        flops=2 * tok * chunk * count * block,
        scratch=[pltpu.VMEM((tok, count * block), bf16)],
    )


def slope_kernel(scale, rate, step, groups, key, pre, up, picked, front, *refs):
    last = groups > 1
    refs, scratch = refs[:-1], refs[-1]
    totals = refs[-groups:]
    share = totals[0].shape[0]
    seen, refs = refs[-1 - groups], refs[: -1 - groups]
    before, carried = (refs[:-1], refs[-1:]) if last else (refs[:-2], refs[-2:])
    chunk = pre.shape[0]
    digits = up[chunk : chunk + 16, :].astype(f32)
    number = digits[0:1] + 256.0 * digits[1:2] + 65536.0 * digits[2:3]
    seen[...] = number + before[0][...] if before else number
    weight = number * rate
    if last:
        norm = 1.0 / seen[...]
    sums = None
    for start in range(0, chunk, step):
        rows = slice(start, start + step)
        slope = slope_of(pre[rows, :], up[rows, :])
        add = jnp.dot(picked[:, rows], slope, preferred_element_type=f32)
        sums = add if sums is None else sums + add
        grad = nt(front[...], slope) * weight[:, :step]
        if before:
            grad += before[1][:, rows]
        if last:
            grad = (grad * norm[:, :step]).astype(bf16)
        for m, total in enumerate(totals):
            total[:, rows] = grad[m * share : (m + 1) * share]
    if last:
        carried[0][...] = (sums * scale).astype(bf16)
    else:
        scratch[...] = sums * scale
        rows = carried[0].shape[0]
        for ref, part in zip(carried, (key[1], 1 - key[1])):
            ref[...] = scratch[pl.ds(pl.multiple_of(part * rows, rows), rows), :].astype(bf16)


def level_two(key, pre, up, picked, front, before, scale, rate, groups):
    chunk, tok = pre.shape
    cols = picked.shape[0]
    step = min(math.gcd(chunk, 256), tok)
    return kernel_call(
        functools.partial(slope_kernel, scale, rate, step, groups),
        ([((cols, tok), bf16)] if groups > 1 else [((cols // 2, tok), bf16)] * 2)
        + [((1, tok), f32)]
        + [((cols // groups, chunk), bf16 if groups > 1 else f32)] * groups,
        [key, pre, up, picked, front] + before,
        flops=4 * tok * cols * chunk,
        scratch=[pltpu.VMEM((cols, tok), f32)],
        exps=tok * chunk,
    )


def add_kernel(*refs):
    total = refs[0][...].astype(f32)
    for ref in refs[1:-1]:
        total += ref[...].astype(f32)
    refs[-1][...] = total.astype(bf16)


def add_up(pieces):
    return kernel_call(add_kernel, [(pieces[0].shape, bf16)], pieces)[0]


def half_kernel(key, *refs):
    halves, (whole, out, total) = refs[:-3], refs[-3:]
    rows = halves[0].shape[0]
    at = pl.ds(pl.multiple_of(key[1] * rows, rows), rows)
    total[...] = whole[...].astype(f32)
    add = halves[0][...].astype(f32)
    for half in halves[1:]:
        add += half[...].astype(f32)
    total[at, :] += add
    out[...] = total[...].astype(bf16)


def add_half(key, pieces):
    shape = pieces[-1].shape
    scratch = [pltpu.VMEM(shape, f32)]
    return kernel_call(half_kernel, [(shape, bf16)], [key] + pieces, scratch=scratch)[0]


def back_kernel(share, mine, theirs, stream, rate, *groups):
    total = stream[...].astype(f32) + mine[...].astype(f32) + theirs[...].astype(f32)
    total = (total * rate[0]).astype(bf16)
    for j, group in enumerate(groups):
        group[...] = total[j * share : (j + 1) * share]


def back_groups(mine, theirs, stream, rate, share):
    cols, tok = stream.shape
    return kernel_call(
        functools.partial(back_kernel, share),
        [((share, tok), bf16)] * (cols // share),
        [mine, theirs, stream, rate],
    )


def hold_kernel(*refs):
    out, start = refs[-1], 0
    for piece in refs[:-1]:
        out[start : start + piece.shape[0], :] = piece[...]
        start += piece.shape[0]


def hold(pieces):
    rows = sum(x.shape[0] for x in pieces)
    return kernel_call(hold_kernel, [((rows, pieces[0].shape[1]), bf16)], pieces)[0]


def part_kernel(*refs):
    groups, (acts, out) = refs[:-2], refs[-2:]
    group = jnp.concatenate([g[...] for g in groups], axis=1)
    out[...] = jnp.dot(group, acts[: group.shape[1], :], preferred_element_type=f32)


def first_part(groups, acts):
    share, hid = groups[0].shape[0], acts.shape[1]
    outs = [((share, hid), f32)]
    flops = 2 * len(groups) * groups[0].size * hid
    return kernel_call(part_kernel, outs, groups + [acts], flops=flops)[0]


def put_out(deltas, steps, piece, moment, outs, bufs, sem):
    copies = []
    for i, at in enumerate(steps):
        for buf, value in zip(bufs, updated(piece[:, at], moment[:, at], deltas(i, at))):
            buf[:, at] = value
        for o, (buf, out) in enumerate(zip(bufs, outs)):
            copies.append(pltpu.make_async_copy(buf.at[:, at], out.at[:, at], sem.at[o, i]))
            copies[-1].start()
    for copy in copies:
        copy.wait()


def finish_kernel(step, *refs):
    refs, (fresh, moment_new, *bufs, sem) = refs[:-5], refs[-5:]
    groups, (acts, done, piece, moment) = refs[:-4], refs[-4:]
    group = jnp.concatenate([g[...] for g in groups], axis=1)
    start = acts.shape[0] - group.shape[1]

    def delta(i, at):
        return done[:, at] + jnp.dot(group, acts[start:, at], preferred_element_type=f32)

    steps = [pl.ds(i, step) for i in range(0, piece.shape[1], step)]
    put_out(delta, steps, piece, moment, (fresh, moment_new), bufs, sem)


def outer_args(shape, count):
    scratch = [pltpu.VMEM(shape, f32)] * 2 + [pltpu.SemaphoreType.DMA((2, count))]
    return dict(outs=[(shape, f32)] * 2, scratch=scratch, outs_in=pl.ANY)


def finish(groups, acts, done, piece, moment):
    _, hid = piece.shape
    step = math.gcd(hid, 1024)
    return kernel_call(
        functools.partial(finish_kernel, step),
        args=groups + [acts, done, piece, moment],
        flops=2 * len(groups) * groups[0].size * hid,
        **outer_args(piece.shape, hid // step),
    )


def outer_kernel(key, piece, moment, *refs):
    deltas, (fresh, moment_new, *bufs, sem) = refs[:-5], refs[-5:]
    chunk = deltas[0].shape[1]
    steps = [
        pl.ds(pl.multiple_of((m ^ key[0]) * chunk, chunk), chunk) for m in range(len(deltas))
    ]
    delta = lambda i, at: deltas[i][...].astype(f32)
    put_out(delta, steps, piece, moment, (fresh, moment_new), bufs, sem)


def outer_chunks(key, piece, moment, deltas):
    args = [key, piece, moment] + deltas
    return kernel_call(outer_kernel, args=args, **outer_args(piece.shape, len(deltas)))


def on_device(
    act_one,
    residual,
    upstream,
    stream_grad,
    token_ids,
    shard_counts,
    out_one,
    in_two,
    out_one_moment,
    in_two_moment,
):
    n_r, n_c, n_t = (lax.axis_size(a) for a in ("row", "col", "tp"))
    r, c, k = (lax.axis_index(a) for a in ("row", "col", "tp"))
    if n_r != n_c or (n_r & (n_r - 1)) or (n_t & (n_t - 1)):
        raise ValueError("mesh")
    act = act_one[0, 0]
    first_store = out_one[0]
    second_store = in_two[0]
    tok, hid = act.shape
    wide = residual.shape[3] * n_t
    cols = stream_grad.shape[3]
    block = wide // n_r
    sub = block // n_t
    chunk = hid // n_c
    share = cols // n_r
    scale_model = 1.0 / math.sqrt(wide)
    scale_hidden = 1.0 / math.sqrt(hid * n_t)
    kernels = n_t == 2 and sub % 128 == 0 and share <= 128 and chunk % 256 == 0

    farthest = sorted(range(1, n_c), reverse=True)
    sent = [part(second_store, c ^ m, chunk, 0) for m in farthest]
    act_out = after(act, *sent)
    weights = {m: swap(piece, "col", m) for m, piece in zip(farthest, sent)}
    mine = after(residual[0, 0], *sent)
    resid_all = [swap(mine, "tp", t) for t in range(n_t)]
    gate = resid_all[-1]
    weights[0] = part(after(second_store, gate), c, chunk, 0)
    acts = {0: [act]}
    for j in sorted(range(1, n_r), key=lambda j: j.bit_count()):
        bits = [1 << b for b in range(n_r.bit_length()) if j >> b & 1]
        if len(bits) == 1:
            acts[j] = [swap(act_out, "row", j)]
        else:
            low, high = bits[0], bits[-1]
            lower = jnp.concatenate(acts[j ^ low])[: tok // 2]
            upper = jnp.concatenate(acts[j ^ high])[tok // 2 :]
            acts[j] = [swap(lower, "row", low), swap(upper, "row", high)]
    keep = (after(token_ids[0, 0], gate) != 0)[:, None]
    up = after(upstream[0, 0], gate)
    up = jnp.where(keep, up, jnp.zeros_like(up)).T
    number = shard_counts[0, 0]
    digits = jnp.stack([(number >> s) & 255 for s in (0, 8, 16)]).astype(bf16)
    digits = jnp.pad(jnp.broadcast_to(digits[:, None], (3, tok)), ((0, 13), (0, 0)))
    sent_ups = [
        jnp.concatenate([part(up, c ^ m, chunk, 0), digits], axis=0) for m in range(n_c)
    ]
    ups = [swap(sent_ups[m], "col", m) for m in range(n_c)]

    resid_all = jnp.stack(resid_all)
    per = wide // n_t
    resid = []
    for j in range(n_r):
        start = (r ^ j) * block + k * sub
        resid.append(
            lax.dynamic_slice(resid_all, ((start // per) ^ k, 0, start % per), (1, tok, sub))[0]
        )

    stream_rows = after(stream_grad[0, 0], gate)
    stream_rows = jnp.where(keep, stream_rows, jnp.zeros_like(stream_rows)).T
    stream_rows = jnp.concatenate(
        arrange([stream_rows[j * share : (j + 1) * share] for j in range(n_r)], r), axis=0
    )
    first = (lambda x: lead(x, share)) if kernels else (lambda x: x[:, :share].T)
    piece_one = first(after(first_store, gate))
    piece_two = first(after(second_store, gate))
    ready = [weights[0], stream_rows, piece_one, piece_two] + resid + sent_ups

    mine = []
    for j in range(n_r):
        behind = ready if j else [gate]
        partial_value = [
            jnp.dot(after(a, *behind), first_store, preferred_element_type=f32)
            for a in acts[j]
        ]
        partial_value = jnp.concatenate([(p * scale_hidden).astype(bf16) for p in partial_value])
        if j == 0:
            ready.append(partial_value)
        summed = part(partial_value, k, sub, 1).astype(f32)
        for t in range(1, n_t):
            summed += swap(part(partial_value, k ^ t, sub, 1), "tp", t).astype(f32)
        mine.append(swap(summed.astype(bf16), "row", j))
    if kernels:
        own = join(resid, mine)
    else:
        own = jnp.concatenate([b.astype(f32) + a.astype(f32) for b, a in zip(resid, mine)], axis=1)
        own = own.astype(bf16)

    count = after(shard_counts[0], own)
    weight_row = [swap(count, "row", j).astype(f32) for j in range(n_r)]
    total_one = sum(weight_row)

    halves = {0: own}
    bit = n_c // 2
    while bit:
        for m in list(halves):
            halves[m | bit] = swap(halves[m], "col", bit)
        bit //= 2
    pieces = [weights[m] for m in range(n_c)]
    key = jnp.stack([c ^ r, k]).astype(jnp.int32)
    if kernels:
        picked = pick(key, pieces, share)
    else:
        picked = jnp.concatenate(arrange([p[:, :share].T for p in pieces], c ^ r), axis=0)
        weight = jnp.concatenate(arrange(pieces, c ^ r), axis=1)

    sums = []
    total_two = 0.0
    arrived = []
    for m in range(n_c):
        streams = [swap(halves[m], "tp", t) for t in range(n_t)]
        if kernels:
            pre, front = pre_second(
                key, streams[0], streams[1], pieces, share, scale_model
            )
            last = m == n_c - 1
            found = level_two(
                key,
                pre,
                ups[m],
                picked,
                front,
                sums,
                scale_model,
                inner_rate * scale_model,
                n_c if last else 1,
            )
            if last:
                carried, grad_two = found[0], found[2:]
            else:
                sums = list(found[2:])
                carried = add_up([found[0], swap(found[1], "tp", 1)])
        else:
            around = arrange([s.reshape(tok, n_r, sub) for s in streams], k)
            stream = jnp.stack(around, axis=2).reshape(tok, wide)
            slope = slope_of(nt(weight, stream) * scale_model, ups[m][:chunk])
            given = ups[m][chunk : chunk + 3, 0].astype(f32)
            given = given[0] + 256.0 * given[1] + 65536.0 * given[2]
            total_two += given
            carried = jnp.dot(picked, slope, preferred_element_type=f32)
            carried = (carried * scale_model).astype(bf16)
            front = stream.reshape(tok, n_c, block)[:, :, :share]
            front = jnp.stack(arrange([front[:, j] for j in range(n_c)], c ^ r), axis=1)
            grad = nt(front.reshape(tok, cols).T, slope) * (given * (inner_rate * scale_model))
            sums.append(grad)
            grad_two = (sum(sums) / total_two).astype(bf16)
            grad_two = [grad_two[m * share : (m + 1) * share] for m in range(n_c)]
        arrived.append(swap(carried, "col", m))

    rate = weight_row[0] * (inner_rate * scale_hidden) / total_one
    if kernels:
        partial_value = add_half(key, arrived)
        theirs = swap(partial_value, "tp", 1)
        groups = back_groups(partial_value, theirs, stream_rows, rate, share)
    else:
        partial_value = sum(a.astype(f32) for a in arrived).astype(bf16)
        back = stream_rows.astype(f32)
        for t in range(n_t):
            back += swap(partial_value, "tp", t).astype(f32)
        back = (back * rate).astype(bf16)
        groups = [back[j * share : (j + 1) * share] for j in range(n_r)]
    groups = [swap(groups[j], "row", j) for j in range(n_r)]

    deltas = [swap(grad_two[m], "col", m) for m in range(n_c)]
    moment_one, moment_two = out_one_moment[0].T, in_two_moment[0].T
    if kernels:
        held = hold([a for j in range(n_r) for a in acts[j]])
        own_key = jnp.stack([c, k]).astype(jnp.int32)
        fresh_two = outer_chunks(own_key, piece_two, moment_two, deltas)
        done = first_part(groups[:1], held)
        fresh_one = finish(groups[1:], held, done, piece_one, moment_one)
    else:
        delta_two = jnp.concatenate(arrange(deltas, c), axis=1).astype(f32)
        fresh_two = updated(piece_two, moment_two, delta_two)
        delta_one = sum(
            jnp.dot(groups[j], jnp.concatenate(acts[j]), preferred_element_type=f32)
            for j in range(n_r)
        )
        fresh_one = updated(piece_one, moment_one, delta_one)
    return tuple(x.T[None] for x in tuple(fresh_one) + tuple(fresh_two))


def solution(mesh):
    return jax.shard_map(
        on_device,
        mesh=mesh,
        in_specs=(
            P("row", "col", None, "tp"),
            P("row", "col", None, "tp"),
            P("row", "col", None, "tp"),
            P("row", "col", None, None),
            P("row", "col", None),
            P("row", "col"),
            P("col", "tp", "row"),
            P("row", "tp", "col"),
            P("col", "tp", "row"),
            P("row", "tp", "col"),
        ),
        out_specs=(
            P("col", "tp", "row"),
            P("col", "tp", "row"),
            P("row", "tp", "col"),
            P("row", "tp", "col"),
        ),
        check_vma=False,
    )
```

```python
import functools
import math

import jax
import jax.numpy as jnp
from jax import lax
from jax.experimental import pallas as pl
from jax.experimental.pallas import tpu as pltpu
from jax.sharding import PartitionSpec as P


inner_rate = 4.0
outer_rate = 0.7
momentum_decay = 0.9


f32 = jnp.float32
bf16 = jnp.bfloat16


def swap(values, axis, step):
    if step == 0:
        return values
    count = lax.axis_size(axis)
    return lax.ppermute(values, axis, [(i, i ^ step) for i in range(count)])


def after(values, *others):
    return lax.optimization_barrier((values,) + others)[0]


def arrange(pieces, key):
    bit = 1
    while bit < len(pieces):
        flip = (key & bit) != 0
        pieces = [jnp.where(flip, pieces[i ^ bit], pieces[i]) for i in range(len(pieces))]
        bit *= 2
    return pieces


def part(values, index, size, dim):
    return lax.dynamic_slice_in_dim(values, index * size, size, dim)


def nt(left, right):
    return lax.dot_general(left, right, (((1,), (1,)), ((), ())), preferred_element_type=f32)


def slope_of(pre, up):
    squash = jax.nn.sigmoid(pre)
    return (up.astype(f32) * squash * (1.0 + pre * (1.0 - squash))).astype(bf16)


def updated(piece, moment, delta):
    moment_new = momentum_decay * moment + delta
    fresh = piece.astype(f32) - outer_rate * (delta + momentum_decay * moment_new)
    return fresh, moment_new


vmem = pl.BlockSpec(memory_space=pltpu.VMEM)
smem = pl.BlockSpec(memory_space=pltpu.SMEM)


def kernel_call(kernel, outs, args, flops=0, scratch=(), exps=0, outs_in=pltpu.VMEM):
    outs = [jax.ShapeDtypeStruct(shape, kind) for shape, kind in outs]
    size = lambda x: math.prod(x.shape) * jnp.dtype(x.dtype).itemsize
    return pl.pallas_call(
        kernel,
        in_specs=[smem if x.size < 16 else vmem for x in args],
        out_specs=[pl.BlockSpec(memory_space=outs_in)] * len(outs),
        out_shape=outs,
        scratch_shapes=list(scratch),
        compiler_params=pltpu.CompilerParams(vmem_limit_bytes=16 << 20),
        cost_estimate=pl.CostEstimate(
            flops=flops,
            bytes_accessed=sum(size(x) for x in outs) + sum(size(x) for x in args),
            transcendentals=exps,
        ),
    )(*args)


def join_kernel(count, *refs):
    base, arrived, out = refs[:count], refs[count : 2 * count], refs[2 * count]
    sub = base[0].shape[1]
    for j in range(count):
        total = base[j][...].astype(f32) + arrived[j][...].astype(f32)
        out[:, j * sub : (j + 1) * sub] = total.astype(bf16)


def join(base, arrived):
    tok, sub = base[0].shape
    count = len(base)
    outs = [((tok, count * sub), bf16)]
    return kernel_call(functools.partial(join_kernel, count), outs, base + arrived)[0]


def pick_kernel(share, key, *refs):
    pieces, out = refs[:-1], refs[-1]
    for m, piece in enumerate(pieces):
        at = pl.ds(pl.multiple_of((m ^ key[0]) * share, share), share)
        out[at, :] = piece[:, :128].T[:share]


def pick(key, pieces, share):
    outs = [((len(pieces) * share, pieces[0].shape[0]), bf16)]
    return kernel_call(functools.partial(pick_kernel, share), outs, [key] + pieces)[0]


def lead_kernel(share, store, out):
    out[...] = store[...].T[:share]


def lead(store, share):
    hid = store.shape[0]
    step = math.gcd(hid, 512)
    return pl.pallas_call(
        functools.partial(lead_kernel, share),
        grid=(hid // step,),
        in_specs=[pl.BlockSpec((step, 128), lambda i: (i, 0))],
        out_specs=pl.BlockSpec((share, step), lambda i: (0, i)),
        out_shape=jax.ShapeDtypeStruct((share, hid), bf16),
        name="lead",
    )(store)


def pre_kernel(scale, share, key, same, other, *refs):
    pieces, (pre, front, stream) = refs[:-3], refs[-3:]
    block = pieces[0].shape[1]
    sub = block // 2
    for m in range(len(pieces)):
        at = pl.ds(pl.multiple_of((m ^ key[0]) * sub, sub), sub)
        mine = m * block + key[1] * sub
        theirs = m * block + (1 - key[1]) * sub
        stream[:, pl.ds(pl.multiple_of(mine, sub), sub)] = same[:, at]
        stream[:, pl.ds(pl.multiple_of(theirs, sub), sub)] = other[:, at]
    for m in range(len(pieces)):
        front[m * share : (m + 1) * share, :] = stream[:, m * block : m * block + 128].T[:share]
    total = nt(pieces[0][...], stream[:, :block])
    for m in range(1, len(pieces)):
        total += nt(pieces[m][...], stream[:, m * block : (m + 1) * block])
    pre[...] = total * scale


def pre_second(key, same, other, pieces, share, scale):
    tok = same.shape[0]
    chunk, block = pieces[0].shape
    count = len(pieces)
    return kernel_call(
        functools.partial(pre_kernel, scale, share),
        [((chunk, tok), f32), ((count * share, tok), bf16)],
        [key, same, other] + pieces,
        flops=2 * tok * chunk * count * block,
        scratch=[pltpu.VMEM((tok, count * block), bf16)],
    )


def slope_kernel(scale, rate, step, groups, key, pre, up, picked, front, *refs):
    last = groups > 1
    refs, scratch = refs[:-1], refs[-1]
    totals = refs[-groups:]
    share = totals[0].shape[0]
    seen, refs = refs[-1 - groups], refs[: -1 - groups]
    before, carried = (refs[:-1], refs[-1:]) if last else (refs[:-2], refs[-2:])
    chunk = pre.shape[0]
    digits = up[chunk : chunk + 16, :].astype(f32)
    number = digits[0:1] + 256.0 * digits[1:2] + 65536.0 * digits[2:3]
    known = number + before[0][0:1] if before else number
    seen[...] = jnp.broadcast_to(known, seen.shape)
    weight = number * rate
    if last:
        norm = 1.0 / known
    sums = None
    for start in range(0, chunk, step):
        rows = slice(start, start + step)
        slope = slope_of(pre[rows, :], up[rows, :])
        add = jnp.dot(picked[:, rows], slope, preferred_element_type=f32)
        sums = add if sums is None else sums + add
        grad = nt(front[...], slope) * weight[:, :step]
        if before:
            grad += before[1][:, rows]
        if last:
            grad = (grad * norm[:, :step]).astype(bf16)
        for m, total in enumerate(totals):
            total[:, rows] = grad[m * share : (m + 1) * share]
    if last:
        carried[0][...] = (sums * scale).astype(bf16)
    else:
        scratch[...] = sums * scale
        rows = carried[0].shape[0]
        for ref, part in zip(carried, (key[1], 1 - key[1])):
            ref[...] = scratch[pl.ds(pl.multiple_of(part * rows, rows), rows), :].astype(bf16)


def level_two(key, pre, up, picked, front, before, scale, rate, groups):
    chunk, tok = pre.shape
    cols = picked.shape[0]
    step = min(math.gcd(chunk, 256), tok)
    return kernel_call(
        functools.partial(slope_kernel, scale, rate, step, groups),
        ([((cols, tok), bf16)] if groups > 1 else [((cols // 2, tok), bf16)] * 2)
        + [((8, tok), f32)]
        + [((cols // groups, chunk), bf16 if groups > 1 else f32)] * groups,
        [key, pre, up, picked, front] + before,
        flops=4 * tok * cols * chunk,
        scratch=[pltpu.VMEM((cols, tok), f32)],
        exps=tok * chunk,
    )


def add_kernel(*refs):
    total = refs[0][...].astype(f32)
    for ref in refs[1:-1]:
        total += ref[...].astype(f32)
    refs[-1][...] = total.astype(bf16)


def add_up(pieces):
    return kernel_call(add_kernel, [(pieces[0].shape, bf16)], pieces)[0]


def half_kernel(key, *refs):
    halves, (whole, out, total) = refs[:-3], refs[-3:]
    rows = halves[0].shape[0]
    at = pl.ds(pl.multiple_of(key[1] * rows, rows), rows)
    total[...] = whole[...].astype(f32)
    add = halves[0][...].astype(f32)
    for half in halves[1:]:
        add += half[...].astype(f32)
    total[at, :] += add
    out[...] = total[...].astype(bf16)


def add_half(key, pieces):
    shape = pieces[-1].shape
    scratch = [pltpu.VMEM(shape, f32)]
    return kernel_call(half_kernel, [(shape, bf16)], [key] + pieces, scratch=scratch)[0]


def back_kernel(share, mine, theirs, stream, rate, *groups):
    total = stream[...].astype(f32) + mine[...].astype(f32) + theirs[...].astype(f32)
    total = (total * rate[0]).astype(bf16)
    for j, group in enumerate(groups):
        group[...] = total[j * share : (j + 1) * share]


def back_groups(mine, theirs, stream, rate, share):
    cols, tok = stream.shape
    return kernel_call(
        functools.partial(back_kernel, share),
        [((share, tok), bf16)] * (cols // share),
        [mine, theirs, stream, rate],
    )


def hold_kernel(*refs):
    out, start = refs[-1], 0
    for piece in refs[:-1]:
        out[start : start + piece.shape[0], :] = piece[...]
        start += piece.shape[0]


def hold(pieces):
    rows = sum(x.shape[0] for x in pieces)
    return kernel_call(hold_kernel, [((rows, pieces[0].shape[1]), bf16)], pieces)[0]


def part_kernel(*refs):
    groups, (acts, out) = refs[:-2], refs[-2:]
    group = jnp.concatenate([g[...] for g in groups], axis=1)
    out[...] = jnp.dot(group, acts[: group.shape[1], :], preferred_element_type=f32)


def first_part(groups, acts):
    share, hid = groups[0].shape[0], acts.shape[1]
    outs = [((share, hid), f32)]
    flops = 2 * len(groups) * groups[0].size * hid
    return kernel_call(part_kernel, outs, groups + [acts], flops=flops)[0]


def put_out(deltas, steps, piece, moment, outs, bufs, sem):
    copies = []
    for i, at in enumerate(steps):
        for buf, value in zip(bufs, updated(piece[:, at], moment[:, at], deltas(i, at))):
            buf[:, at] = value
        for o, (buf, out) in enumerate(zip(bufs, outs)):
            copies.append(pltpu.make_async_copy(buf.at[:, at], out.at[:, at], sem.at[o, i]))
            copies[-1].start()
    for copy in copies:
        copy.wait()


def finish_kernel(step, *refs):
    refs, (fresh, moment_new, *bufs, sem) = refs[:-5], refs[-5:]
    groups, (acts, done, piece, moment) = refs[:-4], refs[-4:]
    group = jnp.concatenate([g[...] for g in groups], axis=1)
    start = acts.shape[0] - group.shape[1]

    def delta(i, at):
        return done[:, at] + jnp.dot(group, acts[start:, at], preferred_element_type=f32)

    steps = [pl.ds(i, step) for i in range(0, piece.shape[1], step)]
    put_out(delta, steps, piece, moment, (fresh, moment_new), bufs, sem)


def outer_args(shape, count):
    scratch = [pltpu.VMEM(shape, f32)] * 2 + [pltpu.SemaphoreType.DMA((2, count))]
    return dict(outs=[(shape, f32)] * 2, scratch=scratch, outs_in=pl.ANY)


def finish(groups, acts, done, piece, moment):
    _, hid = piece.shape
    step = math.gcd(hid, 1024)
    return kernel_call(
        functools.partial(finish_kernel, step),
        args=groups + [acts, done, piece, moment],
        flops=2 * len(groups) * groups[0].size * hid,
        **outer_args(piece.shape, hid // step),
    )


def outer_kernel(key, piece, moment, *refs):
    deltas, (fresh, moment_new, *bufs, sem) = refs[:-5], refs[-5:]
    chunk = deltas[0].shape[1]
    steps = [
        pl.ds(pl.multiple_of((m ^ key[0]) * chunk, chunk), chunk) for m in range(len(deltas))
    ]
    delta = lambda i, at: deltas[i][...].astype(f32)
    put_out(delta, steps, piece, moment, (fresh, moment_new), bufs, sem)


def outer_chunks(key, piece, moment, deltas):
    args = [key, piece, moment] + deltas
    return kernel_call(outer_kernel, args=args, **outer_args(piece.shape, len(deltas)))


def on_device(
    act_one,
    residual,
    upstream,
    stream_grad,
    token_ids,
    shard_counts,
    out_one,
    in_two,
    out_one_moment,
    in_two_moment,
):
    n_r, n_c, n_t = (lax.axis_size(a) for a in ("row", "col", "tp"))
    r, c, k = (lax.axis_index(a) for a in ("row", "col", "tp"))
    if n_r != n_c or (n_r & (n_r - 1)) or (n_t & (n_t - 1)):
        raise ValueError("mesh")
    act = act_one[0, 0]
    first_store = out_one[0]
    second_store = in_two[0]
    tok, hid = act.shape
    wide = residual.shape[3] * n_t
    cols = stream_grad.shape[3]
    block = wide // n_r
    sub = block // n_t
    chunk = hid // n_c
    share = cols // n_r
    scale_model = 1.0 / math.sqrt(wide)
    scale_hidden = 1.0 / math.sqrt(hid * n_t)
    kernels = n_t == 2 and sub % 128 == 0 and share <= 128 and chunk % 256 == 0

    farthest = sorted(range(1, n_c), reverse=True)
    sent = [part(second_store, c ^ farthest[0], chunk, 0)]
    act_out = after(act, sent[0])
    rest = after(second_store, sent[0])
    sent += [part(rest, c ^ m, chunk, 0) for m in farthest[1:]]
    weights = {m: swap(piece, "col", m) for m, piece in zip(farthest, sent)}
    mine = after(residual[0, 0], *sent)
    resid_all = [swap(mine, "tp", t) for t in range(n_t)]
    gate = resid_all[-1]
    weights[0] = part(after(second_store, gate), c, chunk, 0)
    acts = {0: [act]}
    for j in sorted(range(1, n_r), key=lambda j: j.bit_count()):
        bits = [1 << b for b in range(n_r.bit_length()) if j >> b & 1]
        if len(bits) == 1:
            acts[j] = [swap(act_out, "row", j)]
        else:
            low, high = bits[0], bits[-1]
            lower = jnp.concatenate(acts[j ^ low])[: tok // 2]
            upper = jnp.concatenate(acts[j ^ high])[tok // 2 :]
            acts[j] = [swap(lower, "row", low), swap(upper, "row", high)]
    keep = (after(token_ids[0, 0], gate) != 0)[:, None]
    up = after(upstream[0, 0], gate)
    up = jnp.where(keep, up, jnp.zeros_like(up)).T
    number = shard_counts[0, 0]
    digits = jnp.stack([(number >> s) & 255 for s in (0, 8, 16)]).astype(bf16)
    digits = jnp.pad(jnp.broadcast_to(digits[:, None], (3, tok)), ((0, 13), (0, 0)))
    sent_ups = [
        jnp.concatenate([part(up, c ^ m, chunk, 0), digits], axis=0) for m in range(n_c)
    ]
    ups = [swap(sent_ups[m], "col", m) for m in range(n_c)]

    resid_all = jnp.stack(resid_all)
    per = wide // n_t
    resid = []
    for j in range(n_r):
        start = (r ^ j) * block + k * sub
        resid.append(
            lax.dynamic_slice(resid_all, ((start // per) ^ k, 0, start % per), (1, tok, sub))[0]
        )

    stream_rows = after(stream_grad[0, 0], gate)
    stream_rows = jnp.where(keep, stream_rows, jnp.zeros_like(stream_rows)).T
    stream_rows = jnp.concatenate(
        arrange([stream_rows[j * share : (j + 1) * share] for j in range(n_r)], r), axis=0
    )
    first = (lambda x: lead(x, share)) if kernels else (lambda x: x[:, :share].T)
    piece_one = first(after(first_store, gate))
    piece_two = first(after(second_store, gate))
    ready = [weights[0], stream_rows, piece_one, piece_two] + resid + sent_ups

    mine = []
    for j in range(n_r):
        behind = ready if j else [gate]
        partial_value = [
            jnp.dot(after(a, *behind), first_store, preferred_element_type=f32)
            for a in acts[j]
        ]
        partial_value = jnp.concatenate([(p * scale_hidden).astype(bf16) for p in partial_value])
        if j == 0:
            ready.append(partial_value)
        summed = part(partial_value, k, sub, 1).astype(f32)
        for t in range(1, n_t):
            summed += swap(part(partial_value, k ^ t, sub, 1), "tp", t).astype(f32)
        mine.append(swap(summed.astype(bf16), "row", j))
    if kernels:
        own = join(resid, mine)
    else:
        own = jnp.concatenate([b.astype(f32) + a.astype(f32) for b, a in zip(resid, mine)], axis=1)
        own = own.astype(bf16)

    count = after(shard_counts[0], own)
    weight_row = [swap(count, "row", j).astype(f32) for j in range(n_r)]
    total_one = sum(weight_row)

    halves = {0: own}
    bit = n_c // 2
    while bit:
        for m in list(halves):
            halves[m | bit] = swap(halves[m], "col", bit)
        bit //= 2
    pieces = [weights[m] for m in range(n_c)]
    key = jnp.stack([c ^ r, k]).astype(jnp.int32)
    if kernels:
        picked = pick(key, pieces, share)
    else:
        picked = jnp.concatenate(arrange([p[:, :share].T for p in pieces], c ^ r), axis=0)
        weight = jnp.concatenate(arrange(pieces, c ^ r), axis=1)

    sums = []
    total_two = 0.0
    arrived = []
    for m in range(n_c):
        streams = [swap(halves[m], "tp", t) for t in range(n_t)]
        if kernels:
            pre, front = pre_second(
                key, streams[0], streams[1], pieces, share, scale_model
            )
            last = m == n_c - 1
            found = level_two(
                key,
                pre,
                ups[m],
                picked,
                front,
                sums,
                scale_model,
                inner_rate * scale_model,
                n_c if last else 1,
            )
            if last:
                carried, grad_two = found[0], found[2:]
            else:
                sums = list(found[2:])
                carried = add_up([found[0], swap(found[1], "tp", 1)])
        else:
            around = arrange([s.reshape(tok, n_r, sub) for s in streams], k)
            stream = jnp.stack(around, axis=2).reshape(tok, wide)
            slope = slope_of(nt(weight, stream) * scale_model, ups[m][:chunk])
            given = ups[m][chunk : chunk + 3, 0].astype(f32)
            given = given[0] + 256.0 * given[1] + 65536.0 * given[2]
            total_two += given
            carried = jnp.dot(picked, slope, preferred_element_type=f32)
            carried = (carried * scale_model).astype(bf16)
            front = stream.reshape(tok, n_c, block)[:, :, :share]
            front = jnp.stack(arrange([front[:, j] for j in range(n_c)], c ^ r), axis=1)
            grad = nt(front.reshape(tok, cols).T, slope) * (given * (inner_rate * scale_model))
            sums.append(grad)
            grad_two = (sum(sums) / total_two).astype(bf16)
            grad_two = [grad_two[m * share : (m + 1) * share] for m in range(n_c)]
        arrived.append(swap(carried, "col", m))

    rate = weight_row[0] * (inner_rate * scale_hidden) / total_one
    if kernels:
        partial_value = add_half(key, arrived)
        theirs = swap(partial_value, "tp", 1)
        groups = back_groups(partial_value, theirs, stream_rows, rate, share)
    else:
        partial_value = sum(a.astype(f32) for a in arrived).astype(bf16)
        back = stream_rows.astype(f32)
        for t in range(n_t):
            back += swap(partial_value, "tp", t).astype(f32)
        back = (back * rate).astype(bf16)
        groups = [back[j * share : (j + 1) * share] for j in range(n_r)]
    groups = [swap(groups[j], "row", j) for j in range(n_r)]

    deltas = [swap(grad_two[m], "col", m) for m in range(n_c)]
    moment_one, moment_two = out_one_moment[0].T, in_two_moment[0].T
    if kernels:
        held = hold([a for j in range(n_r) for a in acts[j]])
        own_key = jnp.stack([c, k]).astype(jnp.int32)
        fresh_two = outer_chunks(own_key, piece_two, moment_two, deltas)
        done = first_part(groups[:1], held)
        fresh_one = finish(groups[1:], held, done, piece_one, moment_one)
    else:
        delta_two = jnp.concatenate(arrange(deltas, c), axis=1).astype(f32)
        fresh_two = updated(piece_two, moment_two, delta_two)
        delta_one = sum(
            jnp.dot(groups[j], jnp.concatenate(acts[j]), preferred_element_type=f32)
            for j in range(n_r)
        )
        fresh_one = updated(piece_one, moment_one, delta_one)
    return tuple(x.T[None] for x in tuple(fresh_one) + tuple(fresh_two))


def solution(mesh):
    return jax.shard_map(
        on_device,
        mesh=mesh,
        in_specs=(
            P("row", "col", None, "tp"),
            P("row", "col", None, "tp"),
            P("row", "col", None, "tp"),
            P("row", "col", None, None),
            P("row", "col", None),
            P("row", "col"),
            P("col", "tp", "row"),
            P("row", "tp", "col"),
            P("col", "tp", "row"),
            P("row", "tp", "col"),
        ),
        out_specs=(
            P("col", "tp", "row"),
            P("col", "tp", "row"),
            P("row", "tp", "col"),
            P("row", "tp", "col"),
        ),
        check_vma=False,
    )
```
